256 devices in a mesh: grp: 4 (over y), curve: 64 (over z, x, core).
Axes of the slice: x: 4, y: 4, z: 8, core: 2. Of those that a mesh axis runs over, the one named last changes fastest.
Arguments:
- adjoint: float32 [4, 9, 84, 8192], P('grp', None, None, 'curve'), may hold values from -6 to 6
- forward: float32 [2, 4, 9, 84, 8192], P(None, 'grp', None, None, 'curve'), may hold values from -6 to 6
- star_mats: float32 [3, 81, 8192], P(None, None, 'curve'), may hold values from -2 to 2
- flux_own: float32 [4, 81, 8192], P(None, None, 'curve'), may hold values from -2 to 2
- flux_neighbour: float32 [4, 81, 8192], P(None, None, 'curve'), may hold values from -2 to 2
- stiffness: float32 [3, 84, 84], replicated, may hold values from -0.625 to 0.625
- projection: float32 [112, 84], replicated, may hold values from -0.625 to 0.625
- lifting: float32 [4, 84, 28], replicated, may hold values from -0.5 to 0.5
- orientation: float32 [3, 28, 28], replicated, may hold values from -1 to 1
- face_turn: int32 [4, 8192], P(None, 'curve'), may hold values from 0 to 2
- mass_weights: float32 [84], replicated, may hold values from 0.005 to 0.05
- param_mixing: float32 [3, 81], replicated, may hold values from -0.625 to 0.625
- neighbour: int32 [4, 8192], P(None, 'curve'), may hold values from 0 to 768, as said below
- send_map: int32 [2, 8192], P(None, 'curve'), may hold values from 0 to 512, as said below
- element_cell: int32 [8192], P('curve'), may hold values from 0 to 32767, as said below
Outputs:
- adjoint_out: float32 [4, 9, 84, 8192], P('grp', None, None, 'curve')
- kernel_tiles: float32 [256, 3, 128], P(('grp', 'curve'))
The draws below stay inside these ranges and needn't reach their ends.
Inputs may be any that keep to these rules, and one draw needn't show every extreme that they name: `neighbour`: entry [i, c] locates the face adjacent to face i of cell c: below 512 it is the face pointer of a face of the same device, from 512 to 639 a slot sent by the previous device of curve, up to 767 a slot sent by the next device, and 768 a face on the boundary of the slab. `send_map`: each device's block of 128 entries per row holds face pointers of that device's faces in its leading live slots and 512 in the empty ones; at least half of the slots are live, and in each row some device fills all 128. `element_cell`: A cell held by device k of curve lies in a tile u whose position u modulo the number of curve devices is k - 1, k or k + 1; the tile's group u divided by that number may be any.
All inputs are finite; a program needn't handle non-finite values.
Results may differ from the reference program's by a relative error of at most 0.0001.
Values sent between devices are 32-bit elements; how exact they have to be, the bound alone decides.
A program may use at most 128 MiB of HBM per device.

```python
import math
import jax
import jax.numpy as jnp
from jax import lax

BASIS = 84
QUANTITIES = 9
FACE_BASIS = 28
TERMS = 3
STEPS = 2
CELLS = 128
SEND = 128
TOTAL = 8192
TOTAL_SEND = 8192
EVENTS = 4
TILES = 256
INV = 32768
N_CURVE = 64


def draw_neighbour(key, part):
    first, second, third = jax.random.split(jax.random.fold_in(key, 11), 3)
    category = jax.random.randint(first, (4, TOTAL), 0, 26)
    local_face = jax.random.randint(second, (4, TOTAL), 0, 4 * CELLS)
    slot_index = jax.random.randint(third, (4, TOTAL), 0, SEND)
    result = jnp.where(category < 21, local_face, jnp.where(category < 23, 4 * CELLS + slot_index, jnp.where(category < 25, 4 * CELLS + SEND + slot_index, 4 * CELLS + 2 * SEND)))
    return result.astype(jnp.int32)


def draw_send_map(key, part):
    first, second, third = jax.random.split(jax.random.fold_in(key, 23), 3)
    blocks = TOTAL_SEND // SEND
    live_count = jax.random.randint(first, (2, blocks), SEND // 2, SEND + 1)
    chosen = jax.random.randint(second, (2,), 0, blocks)
    live_count = jnp.where(jnp.arange(blocks)[None, :] == chosen[:, None], SEND, live_count)
    faces = jax.random.randint(third, (2, blocks, SEND), 0, 4 * CELLS)
    position = jnp.arange(SEND)[None, None, :]
    result = jnp.where(position < live_count[:, :, None], faces, 4 * CELLS)
    return result.reshape(2, TOTAL_SEND).astype(jnp.int32)


def draw_element_cell(key, part):
    first, second, third = jax.random.split(jax.random.fold_in(key, 37), 3)
    blocks = TOTAL // CELLS
    holder = jnp.arange(TOTAL, dtype=jnp.int32) // CELLS
    group = jax.random.randint(first, (TOTAL,), 0, EVENTS)
    draw_shift = jax.random.randint(second, (TOTAL,), 0, 4)
    shift = jnp.where(draw_shift == 0, -1, jnp.where(draw_shift == 3, 1, 0))
    position = jnp.clip(holder + shift, 0, blocks - 1)
    inside = jax.random.randint(third, (TOTAL,), 0, 128)
    result = (group * blocks + position) * 128 + inside
    result = result.at[0].set(0)
    result = result.at[TOTAL - 1].set(INV - 1)
    return result.astype(jnp.int32)


def plant(values, key, smallest, top_value):
    longest = values.shape.index(max(values.shape))
    spots = []
    for shift in (0, 1):
        where = [jax.random.randint(jax.random.fold_in(key, axis), (), 0, length) for axis, length in enumerate(values.shape)]
        where[longest] = (where[longest] + shift) % values.shape[longest]
        spots.append(tuple(where))
    return values.at[spots[0]].set(smallest).at[spots[1]].set(top_value)


def shard_levels(own_key, extent, pieces, low, largest):
    factor_of, own = 1.0, jax.random.fold_in(own_key, 6)
    for axis_at, parts in pieces:
        steps = jnp.exp(jax.random.uniform(jax.random.fold_in(own, axis_at), (parts,), jnp.float32, low / len(pieces), largest / len(pieces)))
        factor_of = factor_of * jnp.repeat(steps, extent[axis_at] // parts).reshape([-1 if axis == axis_at else 1 for axis in range(len(extent))])
    return factor_of


def centred(key, dims, spread, reach, shards=(), kind=jnp.bfloat16):
    drawn = spread * jax.random.normal(key, dims, jnp.float32)
    if shards:
        drawn = drawn * shard_levels(key, dims, shards, -0.22, 0.18)
    return jnp.clip(drawn, -reach, reach).astype(kind)


def setup_inputs(seed: int = 0) -> dict:
    streams_of = jax.random.split(jax.random.key(seed), 16)
    return {
        "adjoint": centred(streams_of[0], (EVENTS, QUANTITIES, BASIS, TOTAL), 1.0, 6.0, ((0, 4), (3, 64)), jnp.float32),
        "forward": centred(streams_of[1], (STEPS, EVENTS, QUANTITIES, BASIS, TOTAL), 1.0, 6.0, ((1, 4), (4, 64)), jnp.float32),
        "star_mats": centred(streams_of[2], (3, 81, TOTAL), 9 ** -0.5, 2.0, ((2, 64),), jnp.float32),
        "flux_own": centred(streams_of[3], (4, 81, TOTAL), 9 ** -0.5, 2.0, ((2, 64),), jnp.float32),
        "flux_neighbour": centred(streams_of[4], (4, 81, TOTAL), 9 ** -0.5, 2.0, ((2, 64),), jnp.float32),
        "stiffness": centred(streams_of[5], (3, BASIS, BASIS), BASIS ** -0.5, 0.625, (), jnp.float32),
        "projection": centred(streams_of[6], (4 * FACE_BASIS, BASIS), BASIS ** -0.5, 0.625, (), jnp.float32),
        "lifting": centred(streams_of[7], (4, BASIS, FACE_BASIS), (4 * FACE_BASIS) ** -0.5, 0.5, (), jnp.float32),
        "orientation": centred(streams_of[8], (3, FACE_BASIS, FACE_BASIS), FACE_BASIS ** -0.5, 1.0, (), jnp.float32),
        "face_turn": plant(jax.random.randint(streams_of[9], (4, TOTAL), 0, 3), jax.random.fold_in(streams_of[9], 1), 0, 2).astype(jnp.int32),
        "mass_weights": jnp.clip(jnp.exp(jax.random.uniform(streams_of[10], (BASIS,), jnp.float32, math.log(0.005), math.log(0.05))), 0.005, 0.05),
        "param_mixing": centred(streams_of[11], (3, 81), 81 ** -0.5, 0.625, (), jnp.float32),
        "neighbour": draw_neighbour(jax.random.fold_in(streams_of[15], 71), 0),
        "send_map": draw_send_map(jax.random.fold_in(streams_of[15], 71), 0),
        "element_cell": draw_element_cell(jax.random.fold_in(streams_of[15], 71), 0),
    }


PRECISE = lax.Precision.HIGHEST
TIME_STEP = 0.4


def apply_star(matrix, values):
    stacked = []
    for target in range(9):
        summed = matrix[target * 9][None] * values[0]
        for source in range(1, 9):
            summed = summed + matrix[target * 9 + source][None] * values[source]
        stacked.append(summed)
    return jnp.stack(stacked)


def predictor(state, stiffness, star_mats):
    derivative = state
    factor = TIME_STEP
    integral = factor * state
    for degree in range(1, TERMS):
        summed = apply_star(star_mats[0], jnp.einsum('ab,qbc->qac', stiffness[0], derivative, precision=PRECISE))
        for axis_dir in (1, 2):
            summed = summed + apply_star(star_mats[axis_dir], jnp.einsum('ab,qbc->qac', stiffness[axis_dir], derivative, precision=PRECISE))
        derivative = summed
        factor = factor * TIME_STEP / (degree + 1)
        integral = integral + factor * derivative
    return integral


def volume(integral, stiffness, star_mats):
    summed = apply_star(star_mats[0], jnp.einsum('ba,qbc->qac', stiffness[0], integral, precision=PRECISE))
    for axis_dir in (1, 2):
        summed = summed + apply_star(star_mats[axis_dir], jnp.einsum('ba,qbc->qac', stiffness[axis_dir], integral, precision=PRECISE))
    return summed


def turn_faces(gathered, orientation, face_turn):
    result = jnp.zeros_like(gathered)
    for turn_index in range(3):
        turned = jnp.einsum('ts,qsic->qtic', orientation[turn_index], gathered, precision=PRECISE)
        result = result + jnp.where(face_turn[None, None] == turn_index, turned, 0.0)
    return result


def sensitivity(state, forward_state, mass_weights, param_mixing):
    weighted = state * mass_weights[None, :, None]
    correlation = jnp.einsum('qbc,rbc->qrc', weighted, forward_state, precision=PRECISE)
    return jnp.einsum('pk,kc->pc', param_mixing, correlation.reshape(81, -1), precision=PRECISE)


def reference(adjoint, forward, star_mats, flux_own, flux_neighbour, stiffness, projection, lifting, orientation, face_turn, mass_weights, param_mixing, neighbour, send_map, element_cell):
    blocks = N_CURVE
    own_flux = jnp.transpose(flux_own, (1, 0, 2))
    far_flux = jnp.transpose(flux_neighbour, (1, 0, 2))
    sends = send_map.reshape(2, blocks, SEND)
    pointer = jnp.transpose(neighbour.reshape(4, blocks, CELLS), (1, 0, 2)).reshape(blocks, 4 * CELLS)
    flat_index = (element_cell // 128 * 384 + element_cell % 128)[None, :] + 128 * jnp.arange(3, dtype=jnp.int32)[:, None]
    kernel_flat = jnp.zeros((TILES * 384,), jnp.float32)
    blank = jnp.zeros((9, 28, blocks, 1), jnp.float32)
    blank_block = jnp.zeros((9, 28, 1, SEND), jnp.float32)
    finals = []
    for event in range(EVENTS):
        state = adjoint[event]
        for time_step in range(STEPS):
            integral = predictor(state, stiffness, star_mats)
            volume_term = volume(integral, stiffness, star_mats)
            face_traces = jnp.einsum('fb,qbc->qfc', projection, integral, precision=PRECISE)
            own_trace = jnp.transpose(face_traces.reshape(9, 4, 28, TOTAL), (0, 2, 1, 3))
            trace_table = jnp.transpose(face_traces.reshape(9, 4, 28, blocks, CELLS), (0, 2, 3, 1, 4)).reshape(9, 28, blocks, 4 * CELLS)
            padded_table = jnp.concatenate([trace_table, blank], axis=3)
            to_prev = jnp.take_along_axis(padded_table, sends[0][None, None], axis=3)
            to_next = jnp.take_along_axis(padded_table, sends[1][None, None], axis=3)
            from_prev = jnp.concatenate([blank_block, to_next[:, :, :-1]], axis=2)
            from_next = jnp.concatenate([to_prev[:, :, 1:], blank_block], axis=2)
            extended = jnp.concatenate([trace_table, from_prev, from_next, blank], axis=3)
            gathered = jnp.take_along_axis(extended, pointer[None, None], axis=3)
            gathered = jnp.transpose(gathered.reshape(9, 28, blocks, 4, CELLS), (0, 1, 3, 2, 4)).reshape(9, 28, 4, TOTAL)
            oriented = turn_faces(gathered, orientation, face_turn)
            face_flux = apply_star(own_flux, own_trace) + apply_star(far_flux, oriented)
            lifted = jnp.einsum('ibt,qtic->qbc', lifting, face_flux, precision=PRECISE)
            state = state + volume_term - lifted
            density = sensitivity(state, forward[time_step, event], mass_weights, param_mixing)
            kernel_flat = kernel_flat.at[flat_index.reshape(-1)].add(density.reshape(-1))
        finals.append(state)
    return jnp.stack(finals), kernel_flat.reshape(TILES, 3, 128)
```

```python
import jax
import jax.numpy as jnp
from jax import lax
from jax.sharding import PartitionSpec as P

TERMS = 3
STEPS = 2
TILE = 128


PRECISE = lax.Precision.HIGHEST
TIME_STEP = 0.4


def star(matrix, values):
    m3 = matrix.reshape(9, 9, *matrix.shape[1:])
    out = m3[:, 0][:, None] * values[0][None]
    for source in range(1, 9):
        out = out + m3[:, source][:, None] * values[source][None]
    return out


def star_sum(mats, moved):
    out = star(mats[0], moved[0])
    for axis_dir in (1, 2):
        out = out + star(mats[axis_dir], moved[axis_dir])
    return out


def predictor(state, stiffness, star_mats):
    derivative = state
    factor = TIME_STEP
    integral = factor * state
    for degree in range(1, TERMS):
        moved = jnp.einsum("dab,qbc->dqac", stiffness, derivative, precision=PRECISE)
        derivative = star_sum(star_mats, moved)
        factor = factor * TIME_STEP / (degree + 1)
        integral = integral + factor * derivative
    return integral


def volume(integral, stiffness, star_mats):
    moved = jnp.einsum("dba,qbc->dqac", stiffness, integral, precision=PRECISE)
    return star_sum(star_mats, moved)


def turn_faces(gathered, orientation, face_turn):
    turned = jnp.einsum("rts,qsic->rqtic", orientation, gathered, precision=PRECISE)
    result = jnp.zeros_like(gathered)
    for turn_index in range(3):
        result = result + jnp.where(face_turn[None, None] == turn_index, turned[turn_index], 0.0)
    return result


def on_device(
    adjoint,
    forward,
    star_mats,
    flux_own,
    flux_neighbour,
    stiffness,
    projection,
    lifting,
    orientation,
    face_turn,
    mass_weights,
    param_mixing,
    neighbour,
    send_map,
    element_cell,
):
    cells = adjoint.shape[3]
    basis = adjoint.shape[2]
    slots = send_map.shape[1]
    face_basis = projection.shape[0] // 4
    curve_count = lax.axis_size("curve")
    group_count = lax.axis_size("grp")
    my_curve = lax.axis_index("curve")
    my_group = lax.axis_index("grp")
    f32 = jnp.float32

    own_flux = jnp.transpose(flux_own, (1, 0, 2))
    far_flux = jnp.transpose(flux_neighbour, (1, 0, 2))
    face_proj = projection.reshape(4, face_basis, basis)
    rows = 9 * face_basis

    faces = jnp.arange(4 * cells, dtype=jnp.int32)
    send_oh = (faces[:, None] == jnp.concatenate([send_map[0], send_map[1]])[None, :]).astype(f32)
    table_cols = jnp.arange(4 * cells + 2 * slots, dtype=jnp.int32)
    gather_oh = (table_cols[:, None] == neighbour.reshape(-1)[None, :]).astype(f32)

    forward_pairs = [(i, i + 1) for i in range(curve_count - 1)]
    backward_pairs = [(i + 1, i) for i in range(curve_count - 1)]

    mix = param_mixing.reshape(3, 9, 9)
    state = adjoint[0]
    density_sum = jnp.zeros((3, cells), f32)
    for time_step in range(STEPS):
        integral = predictor(state, stiffness, star_mats)
        own_trace = jnp.einsum("itb,qbc->qtic", face_proj, integral, precision=PRECISE)
        table = own_trace.reshape(rows, 4 * cells)
        outgoing = jnp.dot(table, send_oh, precision=PRECISE)
        from_prev = lax.ppermute(outgoing[:, slots:], "curve", forward_pairs)
        from_next = lax.ppermute(outgoing[:, :slots], "curve", backward_pairs)
        volume_term = volume(integral, stiffness, star_mats)
        extended = jnp.concatenate([table, from_prev, from_next], axis=1)
        gathered = jnp.dot(extended, gather_oh, precision=PRECISE).reshape(9, face_basis, 4, cells)
        oriented = turn_faces(gathered, orientation, face_turn)
        face_flux = star(own_flux, own_trace) + star(far_flux, oriented)
        lifted = jnp.einsum("ibt,qtic->qbc", lifting, face_flux, precision=PRECISE)
        state = state + volume_term - lifted
        weighted = state * mass_weights[None, :, None]
        mixed = jnp.einsum("pqr,rbc->pqbc", mix, forward[time_step, 0], precision=PRECISE)
        density_sum = density_sum + jnp.sum(weighted[None] * mixed, axis=(1, 2))

    tile = element_cell // TILE
    inside = element_cell % TILE
    rel_group = (tile // curve_count - my_group) % group_count
    rel_curve = (tile % curve_count - my_curve + 1) % curve_count
    slot = (rel_group * 3 + rel_curve) * TILE + inside
    slot = jnp.where(rel_curve < 3, slot, -1)
    tile_oh = (slot[:, None] == jnp.arange(group_count * 3 * TILE, dtype=jnp.int32)[None, :]).astype(f32)
    partial = jnp.dot(density_sum, tile_oh, precision=PRECISE).reshape(3, group_count, 3, TILE)

    kernel = partial[:, 0, 1]
    for shift_group in range(group_count):
        for shift_curve in (-1, 0, 1):
            if shift_group == 0 and shift_curve == 0:
                continue
            pairs = [
                (
                    g * curve_count + k,
                    ((g + shift_group) % group_count) * curve_count + (k + shift_curve) % curve_count,
                )
                for g in range(group_count)
                for k in range(curve_count)
            ]
            kernel = kernel + lax.ppermute(
                partial[:, shift_group, shift_curve + 1], ("grp", "curve"), pairs
            )
    return (state[None], kernel[None])


def solution(mesh):
    return jax.shard_map(
        on_device,
        mesh=mesh,
        in_specs=(
            P("grp", None, None, "curve"),
            P(None, "grp", None, None, "curve"),
            P(None, None, "curve"),
            P(None, None, "curve"),
            P(None, None, "curve"),
            P(),
            P(),
            P(),
            P(),
            P(None, "curve"),
            P(),
            P(),
            P(None, "curve"),
            P(None, "curve"),
            P("curve"),
        ),
        out_specs=(P("grp", None, None, "curve"), P(("grp", "curve"), None, None)),
        check_vma=False,
    )
```

```python
import jax
import jax.numpy as jnp
from jax import lax
from jax.experimental.layout import Layout, with_layout_constraint
from jax.sharding import PartitionSpec as P

TERMS = 3
STEPS = 2
TILE = 128


PRECISE = lax.Precision.HIGHEST
TIME_STEP = 0.4


def star(matrix, values):
    m3 = matrix.reshape(9, 9, *matrix.shape[1:])
    out = m3[:, 0][:, None] * values[0][None]
    for source in range(1, 9):
        out = out + m3[:, source][:, None] * values[source][None]
    return out


def star_sum(mats, moved):
    out = star(mats[0], moved[0])
    for axis_dir in (1, 2):
        out = out + star(mats[axis_dir], moved[axis_dir])
    return out


def predictor(state, stiffness, star_mats):
    derivative = state
    factor = TIME_STEP
    integral = factor * state
    for degree in range(1, TERMS):
        moved = jnp.einsum("dab,qbc->dqac", stiffness, derivative, precision=PRECISE)
        derivative = star_sum(star_mats, moved)
        factor = factor * TIME_STEP / (degree + 1)
        integral = integral + factor * derivative
    return integral


def volume(integral, stiffness, star_mats):
    moved = jnp.einsum("dba,qbc->dqac", stiffness, integral, precision=PRECISE)
    return star_sum(star_mats, moved)


def turn_faces(gathered, orientation, face_turn):
    turned = jnp.einsum("rts,qsic->rqtic", orientation, gathered, precision=PRECISE)
    result = jnp.zeros_like(gathered)
    for turn_index in range(3):
        result = result + jnp.where(face_turn[None, None] == turn_index, turned[turn_index], 0.0)
    return result


def on_device(
    adjoint,
    forward,
    star_mats,
    flux_own,
    flux_neighbour,
    stiffness,
    projection,
    lifting,
    orientation,
    face_turn,
    mass_weights,
    param_mixing,
    neighbour,
    send_map,
    element_cell,
):
    cells = adjoint.shape[3]
    basis = adjoint.shape[2]
    slots = send_map.shape[1]
    face_basis = projection.shape[0] // 4
    curve_count = lax.axis_size("curve")
    group_count = lax.axis_size("grp")
    my_curve = lax.axis_index("curve")
    my_group = lax.axis_index("grp")
    f32 = jnp.float32

    own_flux = jnp.transpose(flux_own, (1, 0, 2))
    far_flux = jnp.transpose(flux_neighbour, (1, 0, 2))
    face_proj = projection.reshape(4, face_basis, basis)
    rows = 9 * face_basis

    faces = jnp.arange(4 * cells, dtype=jnp.int32)
    send_oh = (faces[:, None] == jnp.concatenate([send_map[0], send_map[1]])[None, :]).astype(f32)
    table_cols = jnp.arange(4 * cells + 2 * slots, dtype=jnp.int32)
    gather_oh = (table_cols[:, None] == neighbour.reshape(-1)[None, :]).astype(f32)

    forward_pairs = [(i, i + 1) for i in range(curve_count - 1)]
    backward_pairs = [(i + 1, i) for i in range(curve_count - 1)]

    mix = param_mixing.reshape(3, 9, 9)
    state = with_layout_constraint(
        adjoint.reshape(adjoint.shape[1:]), Layout((0, 1, 2))
    )
    density_sum = jnp.zeros((3, cells), f32)
    for time_step in range(STEPS):
        integral = predictor(state, stiffness, star_mats)
        own_trace = jnp.einsum("itb,qbc->qtic", face_proj, integral, precision=PRECISE)
        table = own_trace.reshape(rows, 4 * cells)
        outgoing = jnp.dot(table, send_oh, precision=PRECISE)
        from_prev = lax.ppermute(outgoing[:, slots:], "curve", forward_pairs)
        from_next = lax.ppermute(outgoing[:, :slots], "curve", backward_pairs)
        volume_term = volume(integral, stiffness, star_mats)
        extended = jnp.concatenate([table, from_prev, from_next], axis=1)
        gathered = jnp.dot(extended, gather_oh, precision=PRECISE).reshape(9, face_basis, 4, cells)
        oriented = turn_faces(gathered, orientation, face_turn)
        face_flux = star(own_flux, own_trace) + star(far_flux, oriented)
        lifted = jnp.einsum("ibt,qtic->qbc", lifting, face_flux, precision=PRECISE)
        state = state + volume_term - lifted
        weighted = state * mass_weights[None, :, None]
        mixed = jnp.einsum("pqr,rbc->pqbc", mix, forward[time_step, 0], precision=PRECISE)
        density_sum = density_sum + jnp.sum(weighted[None] * mixed, axis=(1, 2))

    tile = element_cell // TILE
    inside = element_cell % TILE
    rel_group = (tile // curve_count - my_group) % group_count
    rel_curve = (tile % curve_count - my_curve + 1) % curve_count
    slot = (rel_group * 3 + rel_curve) * TILE + inside
    slot = jnp.where(rel_curve < 3, slot, -1)
    tile_oh = (slot[:, None] == jnp.arange(group_count * 3 * TILE, dtype=jnp.int32)[None, :]).astype(f32)
    partial = jnp.dot(density_sum, tile_oh, precision=PRECISE).reshape(3, group_count, 3, TILE)

    from_low = lax.ppermute(partial[:, :, 2], "curve", [(i, (i + 1) % curve_count) for i in range(curve_count)])
    from_high = lax.ppermute(partial[:, :, 0], "curve", [((i + 1) % curve_count, i) for i in range(curve_count)])
    gathered_tiles = partial[:, :, 1] + from_low + from_high
    kernel = gathered_tiles[:, 0]
    for shift_group in range(1, group_count):
        pairs = [(g, (g + shift_group) % group_count) for g in range(group_count)]
        kernel = kernel + lax.ppermute(gathered_tiles[:, shift_group], "grp", pairs)
    return (state.reshape(adjoint.shape), kernel[None])


def solution(mesh):
    return jax.shard_map(
        on_device,
        mesh=mesh,
        in_specs=(
            P("grp", None, None, "curve"),
            P(None, "grp", None, None, "curve"),
            P(None, None, "curve"),
            P(None, None, "curve"),
            P(None, None, "curve"),
            P(),
            P(),
            P(),
            P(),
            P(None, "curve"),
            P(),
            P(),
            P(None, "curve"),
            P(None, "curve"),
            P("curve"),
        ),
        out_specs=(P("grp", None, None, "curve"), P(("grp", "curve"), None, None)),
        check_vma=False,
    )
```

```python
import jax
import jax.numpy as jnp
from jax import lax
from jax.experimental import pallas as pl
from jax.experimental.pallas import tpu as pltpu
from jax.experimental.layout import Layout, with_layout_constraint
from jax.sharding import PartitionSpec as P

TERMS = 3
STEPS = 2
TILE = 128


PRECISE = lax.Precision.HIGHEST
TIME_STEP = 0.4


def star(matrix, values):
    m3 = matrix.reshape(9, 9, *matrix.shape[1:])
    out = m3[:, 0][:, None] * values[0][None]
    for source in range(1, 9):
        out = out + m3[:, source][:, None] * values[source][None]
    return out


def star_sum(mats, moved):
    out = star(mats[0], moved[0])
    for axis_dir in (1, 2):
        out = out + star(mats[axis_dir], moved[axis_dir])
    return out


def predictor(state, stiffness, star_mats):
    derivative = state
    factor = TIME_STEP
    integral = factor * state
    for degree in range(1, TERMS):
        moved = jnp.einsum("dab,qbc->dqac", stiffness, derivative, precision=PRECISE)
        derivative = star_sum(star_mats, moved)
        factor = factor * TIME_STEP / (degree + 1)
        integral = integral + factor * derivative
    return integral


def volume(integral, stiffness, star_mats):
    moved = jnp.einsum("dba,qbc->dqac", stiffness, integral, precision=PRECISE)
    return star_sum(star_mats, moved)


def turn_faces(gathered, orientation, face_turn):
    turned = jnp.einsum("rts,qsic->rqtic", orientation, gathered, precision=PRECISE)
    result = jnp.zeros_like(gathered)
    for turn_index in range(3):
        result = result + jnp.where(face_turn[None, None] == turn_index, turned[turn_index], 0.0)
    return result


def exchange_kernel(count, to_next, to_prev, from_prev, from_next, send_sem, recv_sem):
    group = lax.axis_index("grp")
    me = lax.axis_index("curve")
    right, left = lax.rem(me + 1, count), lax.rem(me + count - 1, count)
    barrier = pltpu.get_barrier_semaphore()
    for side in (left, right):
        pl.semaphore_signal(barrier, inc=1, device_id=(group, side), device_id_type=pl.DeviceIdType.MESH)
    pl.semaphore_wait(barrier, 2)
    copies = [
        pltpu.make_async_remote_copy(
            src_ref=to_next,
            dst_ref=from_prev,
            send_sem=send_sem.at[0],
            recv_sem=recv_sem.at[0],
            device_id=(group, right),
            device_id_type=pl.DeviceIdType.MESH,
        ),
        pltpu.make_async_remote_copy(
            src_ref=to_prev,
            dst_ref=from_next,
            send_sem=send_sem.at[1],
            recv_sem=recv_sem.at[1],
            device_id=(group, left),
            device_id_type=pl.DeviceIdType.MESH,
        ),
    ]
    for copy in copies:
        copy.start()
    for copy in copies:
        copy.wait()


def exchange(to_next, to_prev):
    count = lax.axis_size("curve")
    me = lax.axis_index("curve")
    vmem = pl.BlockSpec(memory_space=pltpu.VMEM)
    from_prev, from_next = pl.pallas_call(
        lambda *refs: exchange_kernel(count, *refs),
        out_shape=(jax.ShapeDtypeStruct(to_next.shape, to_next.dtype),) * 2,
        in_specs=[vmem, vmem],
        out_specs=(vmem, vmem),
        scratch_shapes=[pltpu.SemaphoreType.DMA((2,)), pltpu.SemaphoreType.DMA((2,))],
        compiler_params=pltpu.CompilerParams(collective_id=0, has_side_effects=True),
    )(to_next, to_prev)
    from_prev = jnp.where(me == 0, 0.0, from_prev)
    from_next = jnp.where(me == count - 1, 0.0, from_next)
    return from_prev, from_next


def on_device(
    adjoint,
    forward,
    star_mats,
    flux_own,
    flux_neighbour,
    stiffness,
    projection,
    lifting,
    orientation,
    face_turn,
    mass_weights,
    param_mixing,
    neighbour,
    send_map,
    element_cell,
):
    cells = adjoint.shape[3]
    basis = adjoint.shape[2]
    slots = send_map.shape[1]
    face_basis = projection.shape[0] // 4
    curve_count = lax.axis_size("curve")
    group_count = lax.axis_size("grp")
    my_curve = lax.axis_index("curve")
    my_group = lax.axis_index("grp")
    f32 = jnp.float32

    own_flux = jnp.transpose(flux_own, (1, 0, 2))
    far_flux = jnp.transpose(flux_neighbour, (1, 0, 2))
    face_proj = projection.reshape(4, face_basis, basis)
    rows = 9 * face_basis

    faces = jnp.arange(4 * cells, dtype=jnp.int32)
    send_oh = (faces[:, None] == jnp.concatenate([send_map[0], send_map[1]])[None, :]).astype(f32)
    table_cols = jnp.arange(4 * cells + 2 * slots, dtype=jnp.int32)
    gather_oh = (table_cols[:, None] == neighbour.reshape(-1)[None, :]).astype(f32)

    mix = param_mixing.reshape(3, 9, 9)
    state = with_layout_constraint(
        adjoint.reshape(adjoint.shape[1:]), Layout((0, 1, 2))
    )
    density_sum = jnp.zeros((3, cells), f32)
    for time_step in range(STEPS):
        integral = predictor(state, stiffness, star_mats)
        own_trace = jnp.einsum("itb,qbc->qtic", face_proj, integral, precision=PRECISE)
        table = own_trace.reshape(rows, 4 * cells)
        outgoing = jnp.dot(table, send_oh, precision=PRECISE)
        from_prev, from_next = exchange(outgoing[:, slots:], outgoing[:, :slots])
        volume_term = volume(integral, stiffness, star_mats)
        extended = jnp.concatenate([table, from_prev, from_next], axis=1)
        gathered = jnp.dot(extended, gather_oh, precision=PRECISE).reshape(9, face_basis, 4, cells)
        oriented = turn_faces(gathered, orientation, face_turn)
        face_flux = star(own_flux, own_trace) + star(far_flux, oriented)
        lifted = jnp.einsum("ibt,qtic->qbc", lifting, face_flux, precision=PRECISE)
        state = state + volume_term - lifted
        weighted = state * mass_weights[None, :, None]
        mixed = jnp.einsum("pqr,rbc->pqbc", mix, forward[time_step, 0], precision=PRECISE)
        density_sum = density_sum + jnp.sum(weighted[None] * mixed, axis=(1, 2))

    tile = element_cell // TILE
    inside = element_cell % TILE
    rel_group = (tile // curve_count - my_group) % group_count
    rel_curve = (tile % curve_count - my_curve + 1) % curve_count
    slot = (rel_group * 3 + rel_curve) * TILE + inside
    slot = jnp.where(rel_curve < 3, slot, -1)
    tile_oh = (slot[:, None] == jnp.arange(group_count * 3 * TILE, dtype=jnp.int32)[None, :]).astype(f32)
    partial = jnp.dot(density_sum, tile_oh, precision=PRECISE).reshape(3, group_count, 3, TILE)

    from_low = lax.ppermute(partial[:, :, 2], "curve", [(i, (i + 1) % curve_count) for i in range(curve_count)])
    from_high = lax.ppermute(partial[:, :, 0], "curve", [((i + 1) % curve_count, i) for i in range(curve_count)])
    gathered_tiles = partial[:, :, 1] + from_low + from_high
    kernel = gathered_tiles[:, 0]
    for shift_group in range(1, group_count):
        pairs = [(g, (g + shift_group) % group_count) for g in range(group_count)]
        kernel = kernel + lax.ppermute(gathered_tiles[:, shift_group], "grp", pairs)
    return (state.reshape(adjoint.shape), kernel[None])


def solution(mesh):
    return jax.shard_map(
        on_device,
        mesh=mesh,
        in_specs=(
            P("grp", None, None, "curve"),
            P(None, "grp", None, None, "curve"),
            P(None, None, "curve"),
            P(None, None, "curve"),
            P(None, None, "curve"),
            P(),
            P(),
            P(),
            P(),
            P(None, "curve"),
            P(),
            P(),
            P(None, "curve"),
            P(None, "curve"),
            P("curve"),
        ),
        out_specs=(P("grp", None, None, "curve"), P(("grp", "curve"), None, None)),
        check_vma=False,
    )
```

```python
import jax
import jax.numpy as jnp
from jax import lax
from jax.experimental import pallas as pl
from jax.experimental.pallas import tpu as pltpu
from jax.experimental.layout import Layout, with_layout_constraint
from jax.sharding import PartitionSpec as P

TERMS = 3
STEPS = 2
TILE = 128


PRECISE = lax.Precision.HIGHEST
TIME_STEP = 0.4


def star(matrix, values):
    m3 = matrix.reshape(9, 9, *matrix.shape[1:])
    out = m3[:, 0][:, None] * values[0][None]
    for source in range(1, 9):
        out = out + m3[:, source][:, None] * values[source][None]
    return out


def star_sum(mats, moved):
    out = star(mats[0], moved[0])
    for axis_dir in (1, 2):
        out = out + star(mats[axis_dir], moved[axis_dir])
    return out


def predictor(state, stiffness, star_mats):
    derivative = state
    factor = TIME_STEP
    integral = factor * state
    for degree in range(1, TERMS):
        moved = jnp.einsum("dab,qbc->dqac", stiffness, derivative, precision=PRECISE)
        derivative = star_sum(star_mats, moved)
        factor = factor * TIME_STEP / (degree + 1)
        integral = integral + factor * derivative
    return integral


def volume(integral, stiffness, star_mats):
    moved = jnp.einsum("dba,qbc->dqac", stiffness, integral, precision=PRECISE)
    return star_sum(star_mats, moved)


def turn_faces(gathered, orientation, face_turn):
    turned = jnp.einsum("rts,qsic->rqtic", orientation, gathered, precision=PRECISE)
    result = jnp.zeros_like(gathered)
    for turn_index in range(3):
        result = result + jnp.where(face_turn[None, None] == turn_index, turned[turn_index], 0.0)
    return result


def exchange_kernel(count, to_next, to_prev, from_prev, from_next, send_sem, recv_sem):
    group = lax.axis_index("grp")
    me = lax.axis_index("curve")
    right, left = lax.rem(me + 1, count), lax.rem(me + count - 1, count)
    barrier = pltpu.get_barrier_semaphore()
    for side in (left, right):
        pl.semaphore_signal(barrier, inc=1, device_id=(group, side), device_id_type=pl.DeviceIdType.MESH)
    pl.semaphore_wait(barrier, 2)
    copies = [
        pltpu.make_async_remote_copy(
            src_ref=to_next,
            dst_ref=from_prev,
            send_sem=send_sem.at[0],
            recv_sem=recv_sem.at[0],
            device_id=(group, right),
            device_id_type=pl.DeviceIdType.MESH,
        ),
        pltpu.make_async_remote_copy(
            src_ref=to_prev,
            dst_ref=from_next,
            send_sem=send_sem.at[1],
            recv_sem=recv_sem.at[1],
            device_id=(group, left),
            device_id_type=pl.DeviceIdType.MESH,
        ),
    ]
    for copy in copies:
        copy.start()
    for copy in copies:
        copy.wait()


def exchange(to_next, to_prev):
    count = lax.axis_size("curve")
    me = lax.axis_index("curve")
    vmem = pl.BlockSpec(memory_space=pltpu.VMEM)
    from_prev, from_next = pl.pallas_call(
        lambda *refs: exchange_kernel(count, *refs),
        out_shape=(jax.ShapeDtypeStruct(to_next.shape, to_next.dtype),) * 2,
        in_specs=[vmem, vmem],
        out_specs=(vmem, vmem),
        scratch_shapes=[pltpu.SemaphoreType.DMA((2,)), pltpu.SemaphoreType.DMA((2,))],
        compiler_params=pltpu.CompilerParams(collective_id=0, has_side_effects=True),
    )(to_next, to_prev)
    from_prev = jnp.where(me == 0, 0.0, from_prev)
    from_next = jnp.where(me == count - 1, 0.0, from_next)
    return from_prev, from_next


def scatter_kernel(offsets, group_count, curve_count, chunks, received, send_sem, recv_sem):
    group = lax.axis_index("grp")
    me = lax.axis_index("curve")
    targets = [
        (lax.rem(group + shift_group, group_count), lax.rem(me + shift_curve + curve_count, curve_count))
        for shift_group, shift_curve in offsets
    ]
    barrier = pltpu.get_barrier_semaphore()
    for target in targets:
        pl.semaphore_signal(barrier, inc=1, device_id=target, device_id_type=pl.DeviceIdType.MESH)
    pl.semaphore_wait(barrier, len(offsets))
    copies = [
        pltpu.make_async_remote_copy(
            src_ref=chunks.at[index],
            dst_ref=received.at[index],
            send_sem=send_sem.at[index],
            recv_sem=recv_sem.at[index],
            device_id=target,
            device_id_type=pl.DeviceIdType.MESH,
        )
        for index, target in enumerate(targets)
    ]
    for copy in copies:
        copy.start()
    for copy in copies:
        copy.wait()


def scatter_tiles(partial):
    group_count = lax.axis_size("grp")
    curve_count = lax.axis_size("curve")
    offsets = [
        (shift_group, shift_curve)
        for shift_group in range(group_count)
        for shift_curve in (-1, 0, 1)
        if (shift_group, shift_curve) != (0, 0)
    ]
    chunks = jnp.stack([partial[:, g, c + 1] for g, c in offsets])
    vmem = pl.BlockSpec(memory_space=pltpu.VMEM)
    received = pl.pallas_call(
        lambda *refs: scatter_kernel(offsets, group_count, curve_count, *refs),
        out_shape=jax.ShapeDtypeStruct(chunks.shape, chunks.dtype),
        in_specs=[vmem],
        out_specs=vmem,
        scratch_shapes=[
            pltpu.SemaphoreType.DMA((len(offsets),)),
            pltpu.SemaphoreType.DMA((len(offsets),)),
        ],
        compiler_params=pltpu.CompilerParams(collective_id=1, has_side_effects=True),
    )(chunks)
    return partial[:, 0, 1] + jnp.sum(received, axis=0)


def on_device(
    adjoint,
    forward,
    star_mats,
    flux_own,
    flux_neighbour,
    stiffness,
    projection,
    lifting,
    orientation,
    face_turn,
    mass_weights,
    param_mixing,
    neighbour,
    send_map,
    element_cell,
):
    cells = adjoint.shape[3]
    basis = adjoint.shape[2]
    slots = send_map.shape[1]
    face_basis = projection.shape[0] // 4
    curve_count = lax.axis_size("curve")
    group_count = lax.axis_size("grp")
    my_curve = lax.axis_index("curve")
    my_group = lax.axis_index("grp")
    f32 = jnp.float32

    own_flux = jnp.transpose(flux_own, (1, 0, 2))
    far_flux = jnp.transpose(flux_neighbour, (1, 0, 2))
    face_proj = projection.reshape(4, face_basis, basis)
    rows = 9 * face_basis

    faces = jnp.arange(4 * cells, dtype=jnp.int32)
    send_oh = (faces[:, None] == jnp.concatenate([send_map[0], send_map[1]])[None, :]).astype(f32)
    table_cols = jnp.arange(4 * cells + 2 * slots, dtype=jnp.int32)
    gather_oh = (table_cols[:, None] == neighbour.reshape(-1)[None, :]).astype(f32)

    mix = param_mixing.reshape(3, 9, 9)
    state = with_layout_constraint(
        adjoint.reshape(adjoint.shape[1:]), Layout((0, 1, 2))
    )
    density_sum = jnp.zeros((3, cells), f32)
    for time_step in range(STEPS):
        integral = predictor(state, stiffness, star_mats)
        own_trace = jnp.einsum("itb,qbc->qtic", face_proj, integral, precision=PRECISE)
        table = own_trace.reshape(rows, 4 * cells)
        outgoing = jnp.dot(table, send_oh, precision=PRECISE)
        from_prev, from_next = exchange(outgoing[:, slots:], outgoing[:, :slots])
        volume_term = volume(integral, stiffness, star_mats)
        extended = jnp.concatenate([table, from_prev, from_next], axis=1)
        gathered = jnp.dot(extended, gather_oh, precision=PRECISE).reshape(9, face_basis, 4, cells)
        oriented = turn_faces(gathered, orientation, face_turn)
        face_flux = star(own_flux, own_trace) + star(far_flux, oriented)
        lifted = jnp.einsum("ibt,qtic->qbc", lifting, face_flux, precision=PRECISE)
        state = state + volume_term - lifted
        weighted = state * mass_weights[None, :, None]
        mixed = jnp.einsum("pqr,rbc->pqbc", mix, forward[time_step, 0], precision=PRECISE)
        density_sum = density_sum + jnp.sum(weighted[None] * mixed, axis=(1, 2))

    tile = element_cell // TILE
    inside = element_cell % TILE
    rel_group = (tile // curve_count - my_group) % group_count
    rel_curve = (tile % curve_count - my_curve + 1) % curve_count
    slot = (rel_group * 3 + rel_curve) * TILE + inside
    slot = jnp.where(rel_curve < 3, slot, -1)
    tile_oh = (slot[:, None] == jnp.arange(group_count * 3 * TILE, dtype=jnp.int32)[None, :]).astype(f32)
    partial = jnp.dot(density_sum, tile_oh, precision=PRECISE).reshape(3, group_count, 3, TILE)

    kernel = scatter_tiles(partial)
    return (state.reshape(adjoint.shape), kernel[None])


def solution(mesh):
    return jax.shard_map(
        on_device,
        mesh=mesh,
        in_specs=(
            P("grp", None, None, "curve"),
            P(None, "grp", None, None, "curve"),
            P(None, None, "curve"),
            P(None, None, "curve"),
            P(None, None, "curve"),
            P(),
            P(),
            P(),
            P(),
            P(None, "curve"),
            P(),
            P(),
            P(None, "curve"),
            P(None, "curve"),
            P("curve"),
        ),
        out_specs=(P("grp", None, None, "curve"), P(("grp", "curve"), None, None)),
        check_vma=False,
    )
```

```python
import jax
import jax.numpy as jnp
from jax import lax
from jax.experimental import pallas as pl
from jax.experimental.pallas import tpu as pltpu
from jax.experimental.layout import Layout, with_layout_constraint
from jax.sharding import PartitionSpec as P

TERMS = 3
STEPS = 2
TILE = 128


PRECISE = lax.Precision.HIGHEST
DENSE = lax.Precision.HIGH
TIME_STEP = 0.4


def star(matrix, values):
    m3 = matrix.reshape(9, 9, *matrix.shape[1:])
    out = m3[:, 0][:, None] * values[0][None]
    for source in range(1, 9):
        out = out + m3[:, source][:, None] * values[source][None]
    return out


def star_sum(mats, moved):
    out = star(mats[0], moved[0])
    for axis_dir in (1, 2):
        out = out + star(mats[axis_dir], moved[axis_dir])
    return out


def predictor(state, stiffness, star_mats):
    derivative = state
    factor = TIME_STEP
    integral = factor * state
    for degree in range(1, TERMS):
        moved = jnp.einsum("dab,qbc->dqac", stiffness, derivative, precision=DENSE)
        derivative = star_sum(star_mats, moved)
        factor = factor * TIME_STEP / (degree + 1)
        integral = integral + factor * derivative
    return integral


def volume(integral, stiffness, star_mats):
    moved = jnp.einsum("dba,qbc->dqac", stiffness, integral, precision=DENSE)
    return star_sum(star_mats, moved)


def turn_faces(gathered, orientation, face_turn):
    turned = jnp.einsum("rts,qsic->rqtic", orientation, gathered, precision=DENSE)
    result = jnp.zeros_like(gathered)
    for turn_index in range(3):
        result = result + jnp.where(face_turn[None, None] == turn_index, turned[turn_index], 0.0)
    return result


def exchange_kernel(count, to_next, to_prev, from_prev, from_next, send_sem, recv_sem):
    group = lax.axis_index("grp")
    me = lax.axis_index("curve")
    right, left = lax.rem(me + 1, count), lax.rem(me + count - 1, count)
    barrier = pltpu.get_barrier_semaphore()
    for side in (left, right):
        pl.semaphore_signal(barrier, inc=1, device_id=(group, side), device_id_type=pl.DeviceIdType.MESH)
    pl.semaphore_wait(barrier, 2)
    copies = [
        pltpu.make_async_remote_copy(
            src_ref=to_next,
            dst_ref=from_prev,
            send_sem=send_sem.at[0],
            recv_sem=recv_sem.at[0],
            device_id=(group, right),
            device_id_type=pl.DeviceIdType.MESH,
        ),
        pltpu.make_async_remote_copy(
            src_ref=to_prev,
            dst_ref=from_next,
            send_sem=send_sem.at[1],
            recv_sem=recv_sem.at[1],
            device_id=(group, left),
            device_id_type=pl.DeviceIdType.MESH,
        ),
    ]
    for copy in copies:
        copy.start()
    for copy in copies:
        copy.wait()


def exchange(to_next, to_prev):
    count = lax.axis_size("curve")
    me = lax.axis_index("curve")
    vmem = pl.BlockSpec(memory_space=pltpu.VMEM)
    from_prev, from_next = pl.pallas_call(
        lambda *refs: exchange_kernel(count, *refs),
        out_shape=(jax.ShapeDtypeStruct(to_next.shape, to_next.dtype),) * 2,
        in_specs=[vmem, vmem],
        out_specs=(vmem, vmem),
        scratch_shapes=[pltpu.SemaphoreType.DMA((2,)), pltpu.SemaphoreType.DMA((2,))],
        compiler_params=pltpu.CompilerParams(collective_id=0, has_side_effects=True),
    )(to_next, to_prev)
    from_prev = jnp.where(me == 0, 0.0, from_prev)
    from_next = jnp.where(me == count - 1, 0.0, from_next)
    return from_prev, from_next


def scatter_kernel(offsets, group_count, curve_count, chunks, received, send_sem, recv_sem):
    group = lax.axis_index("grp")
    me = lax.axis_index("curve")
    targets = [
        (lax.rem(group + shift_group, group_count), lax.rem(me + shift_curve + curve_count, curve_count))
        for shift_group, shift_curve in offsets
    ]
    barrier = pltpu.get_barrier_semaphore()
    for target in targets:
        pl.semaphore_signal(barrier, inc=1, device_id=target, device_id_type=pl.DeviceIdType.MESH)
    pl.semaphore_wait(barrier, len(offsets))
    copies = [
        pltpu.make_async_remote_copy(
            src_ref=chunks.at[index],
            dst_ref=received.at[index],
            send_sem=send_sem.at[index],
            recv_sem=recv_sem.at[index],
            device_id=target,
            device_id_type=pl.DeviceIdType.MESH,
        )
        for index, target in enumerate(targets)
    ]
    for copy in copies:
        copy.start()
    for copy in copies:
        copy.wait()


def scatter_tiles(partial):
    group_count = lax.axis_size("grp")
    curve_count = lax.axis_size("curve")
    offsets = [
        (shift_group, shift_curve)
        for shift_group in range(group_count)
        for shift_curve in (-1, 0, 1)
        if (shift_group, shift_curve) != (0, 0)
    ]
    chunks = jnp.stack([partial[:, g, c + 1] for g, c in offsets])
    vmem = pl.BlockSpec(memory_space=pltpu.VMEM)
    received = pl.pallas_call(
        lambda *refs: scatter_kernel(offsets, group_count, curve_count, *refs),
        out_shape=jax.ShapeDtypeStruct(chunks.shape, chunks.dtype),
        in_specs=[vmem],
        out_specs=vmem,
        scratch_shapes=[
            pltpu.SemaphoreType.DMA((len(offsets),)),
            pltpu.SemaphoreType.DMA((len(offsets),)),
        ],
        compiler_params=pltpu.CompilerParams(collective_id=1, has_side_effects=True),
    )(chunks)
    return partial[:, 0, 1] + jnp.sum(received, axis=0)


def on_device(
    adjoint,
    forward,
    star_mats,
    flux_own,
    flux_neighbour,
    stiffness,
    projection,
    lifting,
    orientation,
    face_turn,
    mass_weights,
    param_mixing,
    neighbour,
    send_map,
    element_cell,
):
    cells = adjoint.shape[3]
    basis = adjoint.shape[2]
    slots = send_map.shape[1]
    face_basis = projection.shape[0] // 4
    curve_count = lax.axis_size("curve")
    group_count = lax.axis_size("grp")
    my_curve = lax.axis_index("curve")
    my_group = lax.axis_index("grp")
    f32 = jnp.float32

    own_flux = jnp.transpose(flux_own, (1, 0, 2))
    far_flux = jnp.transpose(flux_neighbour, (1, 0, 2))
    face_proj = projection.reshape(4, face_basis, basis)
    rows = 9 * face_basis

    faces = jnp.arange(4 * cells, dtype=jnp.int32)
    send_oh = (faces[:, None] == jnp.concatenate([send_map[0], send_map[1]])[None, :]).astype(f32)
    table_cols = jnp.arange(4 * cells + 2 * slots, dtype=jnp.int32)
    gather_oh = (table_cols[:, None] == neighbour.reshape(-1)[None, :]).astype(f32)

    mix = param_mixing.reshape(3, 9, 9)
    state = with_layout_constraint(
        adjoint.reshape(adjoint.shape[1:]), Layout((0, 1, 2))
    )
    density_sum = jnp.zeros((3, cells), f32)
    for time_step in range(STEPS):
        integral = predictor(state, stiffness, star_mats)
        own_trace = jnp.einsum("itb,qbc->qtic", face_proj, integral, precision=DENSE)
        table = own_trace.reshape(rows, 4 * cells)
        outgoing = jnp.dot(table, send_oh, precision=PRECISE)
        from_prev, from_next = exchange(outgoing[:, slots:], outgoing[:, :slots])
        volume_term = volume(integral, stiffness, star_mats)
        extended = jnp.concatenate([table, from_prev, from_next], axis=1)
        gathered = jnp.dot(extended, gather_oh, precision=PRECISE).reshape(9, face_basis, 4, cells)
        oriented = turn_faces(gathered, orientation, face_turn)
        face_flux = star(own_flux, own_trace) + star(far_flux, oriented)
        lifted = jnp.einsum("ibt,qtic->qbc", lifting, face_flux, precision=DENSE)
        state = state + volume_term - lifted
        weighted = state * mass_weights[None, :, None]
        mixed = jnp.einsum("pqr,rbc->pqbc", mix, forward[time_step, 0], precision=DENSE)
        density_sum = density_sum + jnp.sum(weighted[None] * mixed, axis=(1, 2))

    tile = element_cell // TILE
    inside = element_cell % TILE
    rel_group = (tile // curve_count - my_group) % group_count
    rel_curve = (tile % curve_count - my_curve + 1) % curve_count
    slot = (rel_group * 3 + rel_curve) * TILE + inside
    slot = jnp.where(rel_curve < 3, slot, -1)
    tile_oh = (slot[:, None] == jnp.arange(group_count * 3 * TILE, dtype=jnp.int32)[None, :]).astype(f32)
    partial = jnp.dot(density_sum, tile_oh, precision=PRECISE).reshape(3, group_count, 3, TILE)

    kernel = scatter_tiles(partial)
    return (state.reshape(adjoint.shape), kernel[None])


def solution(mesh):
    return jax.shard_map(
        on_device,
        mesh=mesh,
        in_specs=(
            P("grp", None, None, "curve"),
            P(None, "grp", None, None, "curve"),
            P(None, None, "curve"),
            P(None, None, "curve"),
            P(None, None, "curve"),
            P(),
            P(),
            P(),
            P(),
            P(None, "curve"),
            P(),
            P(),
            P(None, "curve"),
            P(None, "curve"),
            P("curve"),
        ),
        out_specs=(P("grp", None, None, "curve"), P(("grp", "curve"), None, None)),
        check_vma=False,
    )
```

```python
import jax
import jax.numpy as jnp
from jax import lax
from jax.experimental import pallas as pl
from jax.experimental.pallas import tpu as pltpu
from jax.experimental.layout import Layout, with_layout_constraint
from jax.sharding import PartitionSpec as P

TERMS = 3
STEPS = 2
TILE = 128


PRECISE = lax.Precision.HIGHEST
DENSE = lax.Precision.HIGH
TIME_STEP = 0.4


def star(matrix, values):
    m3 = matrix.reshape(9, 9, *matrix.shape[1:])
    out = m3[:, 0][:, None] * values[0][None]
    for source in range(1, 9):
        out = out + m3[:, source][:, None] * values[source][None]
    return out


def star_sum(mats, moved):
    out = star(mats[0], moved[0])
    for axis_dir in (1, 2):
        out = out + star(mats[axis_dir], moved[axis_dir])
    return out


def predictor(state, stiffness, star_mats):
    derivative = state
    factor = TIME_STEP
    integral = factor * state
    for degree in range(1, TERMS):
        moved = jnp.einsum("dab,qbc->dqac", stiffness, derivative, precision=DENSE)
        derivative = star_sum(star_mats, moved)
        factor = factor * TIME_STEP / (degree + 1)
        integral = integral + factor * derivative
    return integral


def volume(integral, stiffness, star_mats):
    moved = jnp.einsum("dba,qbc->dqac", stiffness, integral, precision=DENSE)
    return star_sum(star_mats, moved)


def turn_faces(gathered, orientation, face_turn):
    turned = jnp.einsum("rts,qsic->rqtic", orientation, gathered, precision=DENSE)
    result = jnp.zeros_like(gathered)
    for turn_index in range(3):
        result = result + jnp.where(face_turn[None, None] == turn_index, turned[turn_index], 0.0)
    return result


def add_volume(integral, stiff_t, mats, volume_out, axis_dirs):
    for axis_dir in axis_dirs:
        for source in range(9):
            moved = jnp.dot(
                stiff_t[axis_dir], integral[source], precision=PRECISE, preferred_element_type=jnp.float32
            )
            for target in range(9):
                term = mats[axis_dir, pl.ds(9 * target + source, 1), :] * moved
                if axis_dir == 0 and source == 0:
                    volume_out[target] = term
                else:
                    volume_out[target] = volume_out[target] + term


def exchange_kernel(
    count, to_next, to_prev, integral, stiff_t, mats, from_prev, from_next, volume_out, send_sem, recv_sem
):
    group = lax.axis_index("grp")
    me = lax.axis_index("curve")
    right, left = lax.rem(me + 1, count), lax.rem(me + count - 1, count)
    barrier = pltpu.get_barrier_semaphore()
    for side in (left, right):
        pl.semaphore_signal(barrier, inc=1, device_id=(group, side), device_id_type=pl.DeviceIdType.MESH)
    add_volume(integral, stiff_t, mats, volume_out, (0,))
    pl.semaphore_wait(barrier, 2)
    copies = [
        pltpu.make_async_remote_copy(
            src_ref=to_next,
            dst_ref=from_prev,
            send_sem=send_sem.at[0],
            recv_sem=recv_sem.at[0],
            device_id=(group, right),
            device_id_type=pl.DeviceIdType.MESH,
        ),
        pltpu.make_async_remote_copy(
            src_ref=to_prev,
            dst_ref=from_next,
            send_sem=send_sem.at[1],
            recv_sem=recv_sem.at[1],
            device_id=(group, left),
            device_id_type=pl.DeviceIdType.MESH,
        ),
    ]
    for copy in copies:
        copy.start()
    add_volume(integral, stiff_t, mats, volume_out, (1, 2))
    for copy in copies:
        copy.wait()


def exchange(to_next, to_prev, integral, stiff_t, star_mats):
    count = lax.axis_size("curve")
    me = lax.axis_index("curve")
    vmem = pl.BlockSpec(memory_space=pltpu.VMEM)
    from_prev, from_next, volume_term = pl.pallas_call(
        lambda *refs: exchange_kernel(count, *refs),
        out_shape=(
            jax.ShapeDtypeStruct(to_next.shape, to_next.dtype),
            jax.ShapeDtypeStruct(to_next.shape, to_next.dtype),
            jax.ShapeDtypeStruct(integral.shape, integral.dtype),
        ),
        in_specs=[vmem] * 5,
        out_specs=(vmem, vmem, vmem),
        scratch_shapes=[pltpu.SemaphoreType.DMA((2,)), pltpu.SemaphoreType.DMA((2,))],
        compiler_params=pltpu.CompilerParams(collective_id=0, has_side_effects=True),
    )(to_next, to_prev, integral, stiff_t, star_mats)
    from_prev = jnp.where(me == 0, 0.0, from_prev)
    from_next = jnp.where(me == count - 1, 0.0, from_next)
    return from_prev, from_next, volume_term


def scatter_kernel(offsets, group_count, curve_count, chunks, received, send_sem, recv_sem):
    group = lax.axis_index("grp")
    me = lax.axis_index("curve")
    targets = [
        (lax.rem(group + shift_group, group_count), lax.rem(me + shift_curve + curve_count, curve_count))
        for shift_group, shift_curve in offsets
    ]
    barrier = pltpu.get_barrier_semaphore()
    for target in targets:
        pl.semaphore_signal(barrier, inc=1, device_id=target, device_id_type=pl.DeviceIdType.MESH)
    pl.semaphore_wait(barrier, len(offsets))
    copies = [
        pltpu.make_async_remote_copy(
            src_ref=chunks.at[index],
            dst_ref=received.at[index],
            send_sem=send_sem.at[index],
            recv_sem=recv_sem.at[index],
            device_id=target,
            device_id_type=pl.DeviceIdType.MESH,
        )
        for index, target in enumerate(targets)
    ]
    for copy in copies:
        copy.start()
    for copy in copies:
        copy.wait()


def scatter_tiles(partial):
    group_count = lax.axis_size("grp")
    curve_count = lax.axis_size("curve")
    offsets = [
        (shift_group, shift_curve)
        for shift_group in range(group_count)
        for shift_curve in (-1, 0, 1)
        if (shift_group, shift_curve) != (0, 0)
    ]
    chunks = jnp.stack([partial[:, g, c + 1] for g, c in offsets])
    vmem = pl.BlockSpec(memory_space=pltpu.VMEM)
    received = pl.pallas_call(
        lambda *refs: scatter_kernel(offsets, group_count, curve_count, *refs),
        out_shape=jax.ShapeDtypeStruct(chunks.shape, chunks.dtype),
        in_specs=[vmem],
        out_specs=vmem,
        scratch_shapes=[
            pltpu.SemaphoreType.DMA((len(offsets),)),
            pltpu.SemaphoreType.DMA((len(offsets),)),
        ],
        compiler_params=pltpu.CompilerParams(collective_id=1, has_side_effects=True),
    )(chunks)
    return partial[:, 0, 1] + jnp.sum(received, axis=0)


def on_device(
    adjoint,
    forward,
    star_mats,
    flux_own,
    flux_neighbour,
    stiffness,
    projection,
    lifting,
    orientation,
    face_turn,
    mass_weights,
    param_mixing,
    neighbour,
    send_map,
    element_cell,
):
    cells = adjoint.shape[3]
    basis = adjoint.shape[2]
    slots = send_map.shape[1]
    face_basis = projection.shape[0] // 4
    curve_count = lax.axis_size("curve")
    group_count = lax.axis_size("grp")
    my_curve = lax.axis_index("curve")
    my_group = lax.axis_index("grp")
    f32 = jnp.float32

    own_flux = jnp.transpose(flux_own, (1, 0, 2))
    far_flux = jnp.transpose(flux_neighbour, (1, 0, 2))
    face_proj = projection.reshape(4, face_basis, basis)
    rows = 9 * face_basis

    faces = jnp.arange(4 * cells, dtype=jnp.int32)
    send_oh = (faces[:, None] == jnp.concatenate([send_map[0], send_map[1]])[None, :]).astype(f32)
    table_cols = jnp.arange(4 * cells + 2 * slots, dtype=jnp.int32)
    gather_oh = (table_cols[:, None] == neighbour.reshape(-1)[None, :]).astype(f32)

    mix = param_mixing.reshape(3, 9, 9)
    stiff_t = jnp.transpose(stiffness, (0, 2, 1))
    state = with_layout_constraint(
        adjoint.reshape(adjoint.shape[1:]), Layout((0, 1, 2))
    )
    density_sum = jnp.zeros((3, cells), f32)
    for time_step in range(STEPS):
        integral = predictor(state, stiffness, star_mats)
        own_trace = jnp.einsum("itb,qbc->qtic", face_proj, integral, precision=DENSE)
        table = own_trace.reshape(rows, 4 * cells)
        outgoing = jnp.dot(table, send_oh, precision=PRECISE)
        from_prev, from_next, volume_term = exchange(
            outgoing[:, slots:], outgoing[:, :slots], integral, stiff_t, star_mats
        )
        extended = jnp.concatenate([table, from_prev, from_next], axis=1)
        gathered = jnp.dot(extended, gather_oh, precision=PRECISE).reshape(9, face_basis, 4, cells)
        oriented = turn_faces(gathered, orientation, face_turn)
        face_flux = star(own_flux, own_trace) + star(far_flux, oriented)
        lifted = jnp.einsum("ibt,qtic->qbc", lifting, face_flux, precision=DENSE)
        state = state + volume_term - lifted
        weighted = state * mass_weights[None, :, None]
        mixed = jnp.einsum("pqr,rbc->pqbc", mix, forward[time_step, 0], precision=DENSE)
        density_sum = density_sum + jnp.sum(weighted[None] * mixed, axis=(1, 2))

    tile = element_cell // TILE
    inside = element_cell % TILE
    rel_group = (tile // curve_count - my_group) % group_count
    rel_curve = (tile % curve_count - my_curve + 1) % curve_count
    slot = (rel_group * 3 + rel_curve) * TILE + inside
    slot = jnp.where(rel_curve < 3, slot, -1)
    tile_oh = (slot[:, None] == jnp.arange(group_count * 3 * TILE, dtype=jnp.int32)[None, :]).astype(f32)
    partial = jnp.dot(density_sum, tile_oh, precision=PRECISE).reshape(3, group_count, 3, TILE)

    kernel = scatter_tiles(partial)
    return (state.reshape(adjoint.shape), kernel[None])


def solution(mesh):
    return jax.shard_map(
        on_device,
        mesh=mesh,
        in_specs=(
            P("grp", None, None, "curve"),
            P(None, "grp", None, None, "curve"),
            P(None, None, "curve"),
            P(None, None, "curve"),
            P(None, None, "curve"),
            P(),
            P(),
            P(),
            P(),
            P(None, "curve"),
            P(),
            P(),
            P(None, "curve"),
            P(None, "curve"),
            P("curve"),
        ),
        out_specs=(P("grp", None, None, "curve"), P(("grp", "curve"), None, None)),
        check_vma=False,
    )
```

```python
import jax
import jax.numpy as jnp
from jax import lax
from jax.experimental import pallas as pl
from jax.experimental.pallas import tpu as pltpu
from jax.experimental.layout import Layout, with_layout_constraint
from jax.sharding import PartitionSpec as P

TERMS = 3
STEPS = 2
TILE = 128


PRECISE = lax.Precision.HIGHEST
DENSE = lax.Precision.HIGH
TIME_STEP = 0.4


def star(matrix, values):
    m3 = matrix.reshape(9, 9, *matrix.shape[1:])
    out = m3[:, 0][:, None] * values[0][None]
    for source in range(1, 9):
        out = out + m3[:, source][:, None] * values[source][None]
    return out


def star_sum(mats, moved):
    out = star(mats[0], moved[0])
    for axis_dir in (1, 2):
        out = out + star(mats[axis_dir], moved[axis_dir])
    return out


def predictor(state, stiffness, star_mats):
    derivative = state
    factor = TIME_STEP
    integral = factor * state
    for degree in range(1, TERMS):
        moved = jnp.einsum("dab,qbc->dqac", stiffness, derivative, precision=DENSE)
        derivative = star_sum(star_mats, moved)
        factor = factor * TIME_STEP / (degree + 1)
        integral = integral + factor * derivative
    return integral


def volume(integral, stiffness, star_mats):
    moved = jnp.einsum("dba,qbc->dqac", stiffness, integral, precision=DENSE)
    return star_sum(star_mats, moved)


def turn_faces(gathered, orientation, face_turn):
    turned = jnp.einsum("rts,qsic->rqtic", orientation, gathered, precision=DENSE)
    result = jnp.zeros_like(gathered)
    for turn_index in range(3):
        result = result + jnp.where(face_turn[None, None] == turn_index, turned[turn_index], 0.0)
    return result


def add_volume(integral, stiff_t, mats, volume_out, axis_dirs):
    for axis_dir in axis_dirs:
        for source in range(9):
            moved = jnp.dot(
                stiff_t[axis_dir], integral[source], precision=PRECISE, preferred_element_type=jnp.float32
            )
            for target in range(9):
                term = mats[axis_dir, pl.ds(9 * target + source, 1), :] * moved
                if axis_dir == 0 and source == 0:
                    volume_out[target] = term
                else:
                    volume_out[target] = volume_out[target] + term


def exchange_kernel(
    count, to_next, to_prev, integral, stiff_t, mats, from_prev, from_next, volume_out, send_sem, recv_sem
):
    group = lax.axis_index("grp")
    me = lax.axis_index("curve")
    right, left = lax.rem(me + 1, count), lax.rem(me + count - 1, count)
    barrier = pltpu.get_barrier_semaphore()
    for side in (left, right):
        pl.semaphore_signal(barrier, inc=1, device_id=(group, side), device_id_type=pl.DeviceIdType.MESH)
    add_volume(integral, stiff_t, mats, volume_out, (0,))
    pl.semaphore_wait(barrier, 2)
    copies = [
        pltpu.make_async_remote_copy(
            src_ref=to_next,
            dst_ref=from_prev,
            send_sem=send_sem.at[0],
            recv_sem=recv_sem.at[0],
            device_id=(group, right),
            device_id_type=pl.DeviceIdType.MESH,
        ),
        pltpu.make_async_remote_copy(
            src_ref=to_prev,
            dst_ref=from_next,
            send_sem=send_sem.at[1],
            recv_sem=recv_sem.at[1],
            device_id=(group, left),
            device_id_type=pl.DeviceIdType.MESH,
        ),
    ]
    for copy in copies:
        copy.start()
    add_volume(integral, stiff_t, mats, volume_out, (1, 2))
    for copy in copies:
        copy.wait()


def exchange(to_next, to_prev, integral, stiff_t, star_mats):
    count = lax.axis_size("curve")
    me = lax.axis_index("curve")
    vmem = pl.BlockSpec(memory_space=pltpu.VMEM)
    from_prev, from_next, volume_term = pl.pallas_call(
        lambda *refs: exchange_kernel(count, *refs),
        out_shape=(
            jax.ShapeDtypeStruct(to_next.shape, to_next.dtype),
            jax.ShapeDtypeStruct(to_next.shape, to_next.dtype),
            jax.ShapeDtypeStruct(integral.shape, integral.dtype),
        ),
        in_specs=[vmem] * 5,
        out_specs=(vmem, vmem, vmem),
        scratch_shapes=[pltpu.SemaphoreType.DMA((2,)), pltpu.SemaphoreType.DMA((2,))],
        compiler_params=pltpu.CompilerParams(collective_id=0, has_side_effects=True),
    )(to_next, to_prev, integral, stiff_t, star_mats)
    from_prev = jnp.where(me == 0, 0.0, from_prev)
    from_next = jnp.where(me == count - 1, 0.0, from_next)
    return from_prev, from_next, volume_term


def scatter_kernel(
    offsets, group_count, curve_count,
    state, weights, mixed, earlier, tile_oh, own, received, density, chunks, send_sem, recv_sem,
):
    group = lax.axis_index("grp")
    me = lax.axis_index("curve")
    targets = [
        (lax.rem(group + shift_group, group_count), lax.rem(me + shift_curve + curve_count, curve_count))
        for shift_group, shift_curve in offsets
    ]
    barrier = pltpu.get_barrier_semaphore()
    for target in targets:
        pl.semaphore_signal(barrier, inc=1, device_id=target, device_id_type=pl.DeviceIdType.MESH)
    density[...] = jnp.zeros_like(density)
    for param in range(3):
        summed = earlier[pl.ds(param, 1), :]
        for quantity in range(9):
            weighted = state[quantity] * weights[...]
            summed = summed + jnp.sum(weighted * mixed[param, quantity], axis=0, keepdims=True)
        density[pl.ds(param, 1), :] = summed
    partial = jnp.dot(density[...], tile_oh[...], precision=PRECISE, preferred_element_type=jnp.float32)
    tile = own.shape[1]
    own[...] = partial[:3, tile : 2 * tile]
    for index, (shift_group, shift_curve) in enumerate(offsets):
        start = (shift_group * 3 + shift_curve + 1) * tile
        chunks[index] = partial[:3, start : start + tile]
    pl.semaphore_wait(barrier, len(offsets))
    copies = [
        pltpu.make_async_remote_copy(
            src_ref=chunks.at[index],
            dst_ref=received.at[index],
            send_sem=send_sem.at[index],
            recv_sem=recv_sem.at[index],
            device_id=target,
            device_id_type=pl.DeviceIdType.MESH,
        )
        for index, target in enumerate(targets)
    ]
    for copy in copies:
        copy.start()
    for copy in copies:
        copy.wait()


def scatter_tiles(state, weights, mixed, earlier, tile_oh):
    group_count = lax.axis_size("grp")
    curve_count = lax.axis_size("curve")
    offsets = [
        (shift_group, shift_curve)
        for shift_group in range(group_count)
        for shift_curve in (-1, 0, 1)
        if (shift_group, shift_curve) != (0, 0)
    ]
    cells = state.shape[2]
    vmem = pl.BlockSpec(memory_space=pltpu.VMEM)
    own, received = pl.pallas_call(
        lambda *refs: scatter_kernel(offsets, group_count, curve_count, *refs),
        out_shape=(
            jax.ShapeDtypeStruct((3, TILE), jnp.float32),
            jax.ShapeDtypeStruct((len(offsets), 3, TILE), jnp.float32),
        ),
        in_specs=[vmem] * 5,
        out_specs=(vmem, vmem),
        scratch_shapes=[
            pltpu.VMEM((8, cells), jnp.float32),
            pltpu.VMEM((len(offsets), 3, TILE), jnp.float32),
            pltpu.SemaphoreType.DMA((len(offsets),)),
            pltpu.SemaphoreType.DMA((len(offsets),)),
        ],
        compiler_params=pltpu.CompilerParams(collective_id=1, has_side_effects=True),
    )(state, weights, mixed, earlier, tile_oh)
    return own + jnp.sum(received, axis=0)


def on_device(
    adjoint,
    forward,
    star_mats,
    flux_own,
    flux_neighbour,
    stiffness,
    projection,
    lifting,
    orientation,
    face_turn,
    mass_weights,
    param_mixing,
    neighbour,
    send_map,
    element_cell,
):
    cells = adjoint.shape[3]
    basis = adjoint.shape[2]
    slots = send_map.shape[1]
    face_basis = projection.shape[0] // 4
    curve_count = lax.axis_size("curve")
    group_count = lax.axis_size("grp")
    my_curve = lax.axis_index("curve")
    my_group = lax.axis_index("grp")
    f32 = jnp.float32

    own_flux = jnp.transpose(flux_own, (1, 0, 2))
    far_flux = jnp.transpose(flux_neighbour, (1, 0, 2))
    face_proj = projection.reshape(4, face_basis, basis)
    rows = 9 * face_basis

    faces = jnp.arange(4 * cells, dtype=jnp.int32)
    send_oh = (faces[:, None] == jnp.concatenate([send_map[0], send_map[1]])[None, :]).astype(f32)
    table_cols = jnp.arange(4 * cells + 2 * slots, dtype=jnp.int32)
    gather_oh = (table_cols[:, None] == neighbour.reshape(-1)[None, :]).astype(f32)

    mix = param_mixing.reshape(3, 9, 9)
    stiff_t = jnp.transpose(stiffness, (0, 2, 1))
    state = with_layout_constraint(
        adjoint.reshape(adjoint.shape[1:]), Layout((0, 1, 2))
    )
    density_sum = jnp.zeros((3, cells), f32)
    for time_step in range(STEPS):
        integral = predictor(state, stiffness, star_mats)
        own_trace = jnp.einsum("itb,qbc->qtic", face_proj, integral, precision=DENSE)
        table = own_trace.reshape(rows, 4 * cells)
        outgoing = jnp.dot(table, send_oh, precision=PRECISE)
        from_prev, from_next, volume_term = exchange(
            outgoing[:, slots:], outgoing[:, :slots], integral, stiff_t, star_mats
        )
        extended = jnp.concatenate([table, from_prev, from_next], axis=1)
        gathered = jnp.dot(extended, gather_oh, precision=PRECISE).reshape(9, face_basis, 4, cells)
        oriented = turn_faces(gathered, orientation, face_turn)
        face_flux = star(own_flux, own_trace) + star(far_flux, oriented)
        lifted = jnp.einsum("ibt,qtic->qbc", lifting, face_flux, precision=DENSE)
        state = state + volume_term - lifted
        mixed = jnp.einsum("pqr,rbc->pqbc", mix, forward[time_step, 0], precision=DENSE)
        if time_step < STEPS - 1:
            weighted = state * mass_weights[None, :, None]
            density_sum = density_sum + jnp.sum(weighted[None] * mixed, axis=(1, 2))

    tile = element_cell // TILE
    inside = element_cell % TILE
    rel_group = (tile // curve_count - my_group) % group_count
    rel_curve = (tile % curve_count - my_curve + 1) % curve_count
    slot = (rel_group * 3 + rel_curve) * TILE + inside
    slot = jnp.where(rel_curve < 3, slot, -1)
    tile_oh = (slot[:, None] == jnp.arange(group_count * 3 * TILE, dtype=jnp.int32)[None, :]).astype(f32)
    kernel = scatter_tiles(state, mass_weights[:, None], mixed, density_sum, tile_oh)
    return (state.reshape(adjoint.shape), kernel[None])


def solution(mesh):
    return jax.shard_map(
        on_device,
        mesh=mesh,
        in_specs=(
            P("grp", None, None, "curve"),
            P(None, "grp", None, None, "curve"),
            P(None, None, "curve"),
            P(None, None, "curve"),
            P(None, None, "curve"),
            P(),
            P(),
            P(),
            P(),
            P(None, "curve"),
            P(),
            P(),
            P(None, "curve"),
            P(None, "curve"),
            P("curve"),
        ),
        out_specs=(P("grp", None, None, "curve"), P(("grp", "curve"), None, None)),
        check_vma=False,
    )
```

```python
import jax
import jax.numpy as jnp
from jax import lax
from jax.experimental import pallas as pl
from jax.experimental.pallas import tpu as pltpu
from jax.experimental.layout import Layout, with_layout_constraint
from jax.sharding import PartitionSpec as P

TERMS = 3
STEPS = 2
TILE = 128


PRECISE = lax.Precision.HIGHEST
DENSE = lax.Precision.HIGH
TIME_STEP = 0.4


def star(matrix, values):
    m3 = matrix.reshape(9, 9, *matrix.shape[1:])
    out = m3[:, 0][:, None] * values[0][None]
    for source in range(1, 9):
        out = out + m3[:, source][:, None] * values[source][None]
    return out


def star_sum(mats, moved):
    out = star(mats[0], moved[0])
    for axis_dir in (1, 2):
        out = out + star(mats[axis_dir], moved[axis_dir])
    return out


def predictor(state, stiffness, star_mats):
    derivative = state
    factor = TIME_STEP
    integral = factor * state
    for degree in range(1, TERMS):
        moved = jnp.einsum("dab,qbc->dqac", stiffness, derivative, precision=DENSE)
        derivative = star_sum(star_mats, moved)
        factor = factor * TIME_STEP / (degree + 1)
        integral = integral + factor * derivative
    return integral


def volume(integral, stiffness, star_mats):
    moved = jnp.einsum("dba,qbc->dqac", stiffness, integral, precision=DENSE)
    return star_sum(star_mats, moved)


def turn_faces(gathered, orientation, face_turn):
    turned = jnp.einsum("rts,qsic->rqtic", orientation, gathered, precision=DENSE)
    result = jnp.zeros_like(gathered)
    for turn_index in range(3):
        result = result + jnp.where(face_turn[None, None] == turn_index, turned[turn_index], 0.0)
    return result


def add_volume(integral, stiff_t, mats, volume_out, axis_dirs):
    for axis_dir in axis_dirs:
        for source in range(9):
            moved = jnp.dot(
                stiff_t[axis_dir], integral[source], precision=PRECISE, preferred_element_type=jnp.float32
            )
            for target in range(9):
                term = mats[axis_dir, pl.ds(9 * target + source, 1), :] * moved
                if axis_dir == 0 and source == 0:
                    volume_out[target] = term
                else:
                    volume_out[target] = volume_out[target] + term


def exchange_kernel(
    count, to_next, to_prev, integral, stiff_t, mats, from_prev, from_next, volume_out, send_sem, recv_sem
):
    group = lax.axis_index("grp")
    me = lax.axis_index("curve")
    has_left = me > 0
    has_right = me < count - 1
    barrier = pltpu.get_barrier_semaphore()

    @pl.when(has_left)
    def _():
        pl.semaphore_signal(barrier, inc=1, device_id=(group, me - 1), device_id_type=pl.DeviceIdType.MESH)

    @pl.when(has_right)
    def _():
        pl.semaphore_signal(barrier, inc=1, device_id=(group, me + 1), device_id_type=pl.DeviceIdType.MESH)

    @pl.when(me == 0)
    def _():
        from_prev[...] = jnp.zeros_like(from_prev)

    @pl.when(me == count - 1)
    def _():
        from_next[...] = jnp.zeros_like(from_next)

    add_volume(integral, stiff_t, mats, volume_out, (0,))
    to_right = pltpu.make_async_remote_copy(
        src_ref=to_next,
        dst_ref=from_prev,
        send_sem=send_sem.at[0],
        recv_sem=recv_sem.at[0],
        device_id=(group, lax.rem(me + 1, count)),
        device_id_type=pl.DeviceIdType.MESH,
    )
    to_left = pltpu.make_async_remote_copy(
        src_ref=to_prev,
        dst_ref=from_next,
        send_sem=send_sem.at[1],
        recv_sem=recv_sem.at[1],
        device_id=(group, lax.rem(me + count - 1, count)),
        device_id_type=pl.DeviceIdType.MESH,
    )

    neighbours = (me + count - 1) // count + (2 * count - 2 - me) // count
    pl.semaphore_wait(barrier, neighbours)

    @pl.when(has_right)
    def _():
        to_right.start()

    @pl.when(has_left)
    def _():
        to_left.start()

    add_volume(integral, stiff_t, mats, volume_out, (1, 2))

    @pl.when(has_right)
    def _():
        to_right.wait_send()
        to_left.wait_recv()

    @pl.when(has_left)
    def _():
        to_left.wait_send()
        to_right.wait_recv()


def exchange(to_next, to_prev, integral, stiff_t, star_mats):
    count = lax.axis_size("curve")
    vmem = pl.BlockSpec(memory_space=pltpu.VMEM)
    return pl.pallas_call(
        lambda *refs: exchange_kernel(count, *refs),
        out_shape=(
            jax.ShapeDtypeStruct(to_next.shape, to_next.dtype),
            jax.ShapeDtypeStruct(to_next.shape, to_next.dtype),
            jax.ShapeDtypeStruct(integral.shape, integral.dtype),
        ),
        in_specs=[vmem] * 5,
        out_specs=(vmem, vmem, vmem),
        scratch_shapes=[pltpu.SemaphoreType.DMA((2,)), pltpu.SemaphoreType.DMA((2,))],
        compiler_params=pltpu.CompilerParams(collective_id=0, has_side_effects=True),
    )(to_next, to_prev, integral, stiff_t, star_mats)


def scatter_kernel(offsets, group_count, curve_count, chunks, received, send_sem, recv_sem):
    group = lax.axis_index("grp")
    me = lax.axis_index("curve")
    targets = [
        (lax.rem(group + shift_group, group_count), lax.rem(me + shift_curve + curve_count, curve_count))
        for shift_group, shift_curve in offsets
    ]
    barrier = pltpu.get_barrier_semaphore()
    for target in targets:
        pl.semaphore_signal(barrier, inc=1, device_id=target, device_id_type=pl.DeviceIdType.MESH)
    pl.semaphore_wait(barrier, len(offsets))
    copies = [
        pltpu.make_async_remote_copy(
            src_ref=chunks.at[index],
            dst_ref=received.at[index],
            send_sem=send_sem.at[index],
            recv_sem=recv_sem.at[index],
            device_id=target,
            device_id_type=pl.DeviceIdType.MESH,
        )
        for index, target in enumerate(targets)
    ]
    for copy in copies:
        copy.start()
    for copy in copies:
        copy.wait()


def scatter_tiles(partial):
    group_count = lax.axis_size("grp")
    curve_count = lax.axis_size("curve")
    offsets = [
        (shift_group, shift_curve)
        for shift_group in range(group_count)
        for shift_curve in (-1, 0, 1)
        if (shift_group, shift_curve) != (0, 0)
    ]
    chunks = jnp.stack([partial[:, g, c + 1] for g, c in offsets])
    vmem = pl.BlockSpec(memory_space=pltpu.VMEM)
    received = pl.pallas_call(
        lambda *refs: scatter_kernel(offsets, group_count, curve_count, *refs),
        out_shape=jax.ShapeDtypeStruct(chunks.shape, chunks.dtype),
        in_specs=[vmem],
        out_specs=vmem,
        scratch_shapes=[
            pltpu.SemaphoreType.DMA((len(offsets),)),
            pltpu.SemaphoreType.DMA((len(offsets),)),
        ],
        compiler_params=pltpu.CompilerParams(collective_id=1, has_side_effects=True),
    )(chunks)
    return partial[:, 0, 1] + jnp.sum(received, axis=0)


def on_device(
    adjoint,
    forward,
    star_mats,
    flux_own,
    flux_neighbour,
    stiffness,
    projection,
    lifting,
    orientation,
    face_turn,
    mass_weights,
    param_mixing,
    neighbour,
    send_map,
    element_cell,
):
    cells = adjoint.shape[3]
    basis = adjoint.shape[2]
    slots = send_map.shape[1]
    face_basis = projection.shape[0] // 4
    curve_count = lax.axis_size("curve")
    group_count = lax.axis_size("grp")
    my_curve = lax.axis_index("curve")
    my_group = lax.axis_index("grp")
    f32 = jnp.float32

    own_flux = jnp.transpose(flux_own, (1, 0, 2))
    far_flux = jnp.transpose(flux_neighbour, (1, 0, 2))
    face_proj = projection.reshape(4, face_basis, basis)
    rows = 9 * face_basis

    faces = jnp.arange(4 * cells, dtype=jnp.int32)
    send_oh = (faces[:, None] == jnp.concatenate([send_map[0], send_map[1]])[None, :]).astype(f32)
    table_cols = jnp.arange(4 * cells + 2 * slots, dtype=jnp.int32)
    gather_oh = (table_cols[:, None] == neighbour.reshape(-1)[None, :]).astype(f32)

    mix = param_mixing.reshape(3, 9, 9)
    stiff_t = jnp.transpose(stiffness, (0, 2, 1))
    state = with_layout_constraint(
        adjoint.reshape(adjoint.shape[1:]), Layout((0, 1, 2))
    )
    density_sum = jnp.zeros((3, cells), f32)
    for time_step in range(STEPS):
        integral = predictor(state, stiffness, star_mats)
        own_trace = jnp.einsum("itb,qbc->qtic", face_proj, integral, precision=DENSE)
        table = own_trace.reshape(rows, 4 * cells)
        outgoing = jnp.dot(table, send_oh, precision=PRECISE)
        from_prev, from_next, volume_term = exchange(
            outgoing[:, slots:], outgoing[:, :slots], integral, stiff_t, star_mats
        )
        extended = jnp.concatenate([table, from_prev, from_next], axis=1)
        gathered = jnp.dot(extended, gather_oh, precision=PRECISE).reshape(9, face_basis, 4, cells)
        oriented = turn_faces(gathered, orientation, face_turn)
        face_flux = star(own_flux, own_trace) + star(far_flux, oriented)
        lifted = jnp.einsum("ibt,qtic->qbc", lifting, face_flux, precision=DENSE)
        state = state + volume_term - lifted
        weighted = state * mass_weights[None, :, None]
        mixed = jnp.einsum("pqr,rbc->pqbc", mix, forward[time_step, 0], precision=DENSE)
        density_sum = density_sum + jnp.sum(weighted[None] * mixed, axis=(1, 2))

    tile = element_cell // TILE
    inside = element_cell % TILE
    rel_group = (tile // curve_count - my_group) % group_count
    rel_curve = (tile % curve_count - my_curve + 1) % curve_count
    slot = (rel_group * 3 + rel_curve) * TILE + inside
    slot = jnp.where(rel_curve < 3, slot, -1)
    tile_oh = (slot[:, None] == jnp.arange(group_count * 3 * TILE, dtype=jnp.int32)[None, :]).astype(f32)
    partial = jnp.dot(density_sum, tile_oh, precision=PRECISE).reshape(3, group_count, 3, TILE)

    kernel = scatter_tiles(partial)
    return (state.reshape(adjoint.shape), kernel[None])


def solution(mesh):
    return jax.shard_map(
        on_device,
        mesh=mesh,
        in_specs=(
            P("grp", None, None, "curve"),
            P(None, "grp", None, None, "curve"),
            P(None, None, "curve"),
            P(None, None, "curve"),
            P(None, None, "curve"),
            P(),
            P(),
            P(),
            P(),
            P(None, "curve"),
            P(),
            P(),
            P(None, "curve"),
            P(None, "curve"),
            P("curve"),
        ),
        out_specs=(P("grp", None, None, "curve"), P(("grp", "curve"), None, None)),
        check_vma=False,
    )
```

```python
import jax
import jax.numpy as jnp
from jax import lax
from jax.experimental import pallas as pl
from jax.experimental.pallas import tpu as pltpu
from jax.experimental.layout import Layout, with_layout_constraint
from jax.sharding import PartitionSpec as P

TERMS = 3
STEPS = 2
TILE = 128


PRECISE = lax.Precision.HIGHEST
DENSE = lax.Precision.HIGH
TIME_STEP = 0.4


def star(matrix, values):
    m3 = matrix.reshape(9, 9, *matrix.shape[1:])
    out = m3[:, 0][:, None] * values[0][None]
    for source in range(1, 9):
        out = out + m3[:, source][:, None] * values[source][None]
    return out


def star_sum(mats, moved):
    out = star(mats[0], moved[0])
    for axis_dir in (1, 2):
        out = out + star(mats[axis_dir], moved[axis_dir])
    return out


def predictor(state, stiffness, star_mats):
    derivative = state
    factor = TIME_STEP
    integral = factor * state
    for degree in range(1, TERMS):
        moved = jnp.einsum("dab,qbc->dqac", stiffness, derivative, precision=DENSE)
        derivative = star_sum(star_mats, moved)
        factor = factor * TIME_STEP / (degree + 1)
        integral = integral + factor * derivative
    return integral


def volume(integral, stiffness, star_mats):
    moved = jnp.einsum("dba,qbc->dqac", stiffness, integral, precision=DENSE)
    return star_sum(star_mats, moved)


def turn_faces(gathered, orientation, face_turn):
    turned = jnp.einsum("rts,qsic->rqtic", orientation, gathered, precision=DENSE)
    result = jnp.zeros_like(gathered)
    for turn_index in range(3):
        result = result + jnp.where(face_turn[None, None] == turn_index, turned[turn_index], 0.0)
    return result


def add_volume(integral, stiff_t, mats, volume_out, axis_dirs):
    for axis_dir in axis_dirs:
        for source in range(9):
            moved = jnp.dot(
                stiff_t[axis_dir], integral[source], precision=PRECISE, preferred_element_type=jnp.float32
            )
            for target in range(9):
                term = mats[axis_dir, pl.ds(9 * target + source, 1), :] * moved
                if axis_dir == 0 and source == 0:
                    volume_out[target] = term
                else:
                    volume_out[target] = volume_out[target] + term


def exchange_kernel(
    count, to_next, to_prev, integral, stiff_t, mats, from_prev, from_next, volume_out, send_sem, recv_sem
):
    group = lax.axis_index("grp")
    me = lax.axis_index("curve")
    has_left = me > 0
    has_right = me < count - 1
    barrier = pltpu.get_barrier_semaphore()

    @pl.when(has_left)
    def _():
        pl.semaphore_signal(barrier, inc=1, device_id=(group, me - 1), device_id_type=pl.DeviceIdType.MESH)

    @pl.when(has_right)
    def _():
        pl.semaphore_signal(barrier, inc=1, device_id=(group, me + 1), device_id_type=pl.DeviceIdType.MESH)

    @pl.when(me == 0)
    def _():
        from_prev[...] = jnp.zeros_like(from_prev)

    @pl.when(me == count - 1)
    def _():
        from_next[...] = jnp.zeros_like(from_next)

    add_volume(integral, stiff_t, mats, volume_out, (0,))
    to_right = pltpu.make_async_remote_copy(
        src_ref=to_next,
        dst_ref=from_prev,
        send_sem=send_sem.at[0],
        recv_sem=recv_sem.at[0],
        device_id=(group, lax.rem(me + 1, count)),
        device_id_type=pl.DeviceIdType.MESH,
    )
    to_left = pltpu.make_async_remote_copy(
        src_ref=to_prev,
        dst_ref=from_next,
        send_sem=send_sem.at[1],
        recv_sem=recv_sem.at[1],
        device_id=(group, lax.rem(me + count - 1, count)),
        device_id_type=pl.DeviceIdType.MESH,
    )

    neighbours = (me + count - 1) // count + (2 * count - 2 - me) // count
    pl.semaphore_wait(barrier, neighbours)

    @pl.when(has_right)
    def _():
        to_right.start()

    @pl.when(has_left)
    def _():
        to_left.start()

    add_volume(integral, stiff_t, mats, volume_out, (1, 2))

    @pl.when(has_right)
    def _():
        to_right.wait_send()
        to_left.wait_recv()

    @pl.when(has_left)
    def _():
        to_left.wait_send()
        to_right.wait_recv()


def exchange(to_next, to_prev, integral, stiff_t, star_mats):
    count = lax.axis_size("curve")
    vmem = pl.BlockSpec(memory_space=pltpu.VMEM)
    return pl.pallas_call(
        lambda *refs: exchange_kernel(count, *refs),
        out_shape=(
            jax.ShapeDtypeStruct(to_next.shape, to_next.dtype),
            jax.ShapeDtypeStruct(to_next.shape, to_next.dtype),
            jax.ShapeDtypeStruct(integral.shape, integral.dtype),
        ),
        in_specs=[vmem] * 5,
        out_specs=(vmem, vmem, vmem),
        scratch_shapes=[pltpu.SemaphoreType.DMA((2,)), pltpu.SemaphoreType.DMA((2,))],
        compiler_params=pltpu.CompilerParams(collective_id=0, has_side_effects=True),
    )(to_next, to_prev, integral, stiff_t, star_mats)


def scatter_kernel(offsets, group_count, curve_count, chunks, received, send_sem, recv_sem):
    group = lax.axis_index("grp")
    me = lax.axis_index("curve")
    sides = {-1: me > 0, 0: None, 1: me < curve_count - 1}
    targets = [
        (lax.rem(group + shift_group, group_count), lax.rem(me + shift_curve + curve_count, curve_count))
        for shift_group, shift_curve in offsets
    ]

    def maybe(side, action):
        if sides[side] is None:
            action()
        else:
            pl.when(sides[side])(action)

    barrier = pltpu.get_barrier_semaphore()
    for (shift_group, shift_curve), target in zip(offsets, targets):
        maybe(
            shift_curve,
            lambda target=target: pl.semaphore_signal(
                barrier, inc=1, device_id=target, device_id_type=pl.DeviceIdType.MESH
            ),
        )
    for index, (shift_group, shift_curve) in enumerate(offsets):
        if shift_curve != 0:

            def clear(index=index):
                received[index] = jnp.zeros_like(received[index])

            pl.when(jnp.logical_not(sides[-shift_curve]))(clear)
    has_left = (me + curve_count - 1) // curve_count
    has_right = (2 * curve_count - 2 - me) // curve_count
    per_side = sum(1 for _, shift_curve in offsets if shift_curve == 1)
    steady = sum(1 for _, shift_curve in offsets if shift_curve == 0)
    pl.semaphore_wait(barrier, steady + per_side * (has_left + has_right))
    copies = [
        pltpu.make_async_remote_copy(
            src_ref=chunks.at[index],
            dst_ref=received.at[index],
            send_sem=send_sem.at[index],
            recv_sem=recv_sem.at[index],
            device_id=target,
            device_id_type=pl.DeviceIdType.MESH,
        )
        for index, target in enumerate(targets)
    ]
    for (shift_group, shift_curve), copy in zip(offsets, copies):
        maybe(shift_curve, copy.start)
    for (shift_group, shift_curve), copy in zip(offsets, copies):
        maybe(shift_curve, copy.wait_send)
        maybe(-shift_curve, copy.wait_recv)


def scatter_tiles(partial):
    group_count = lax.axis_size("grp")
    curve_count = lax.axis_size("curve")
    offsets = [
        (shift_group, shift_curve)
        for shift_group in range(group_count)
        for shift_curve in (-1, 0, 1)
        if (shift_group, shift_curve) != (0, 0)
    ]
    chunks = jnp.stack([partial[:, g, c + 1] for g, c in offsets])
    vmem = pl.BlockSpec(memory_space=pltpu.VMEM)
    received = pl.pallas_call(
        lambda *refs: scatter_kernel(offsets, group_count, curve_count, *refs),
        out_shape=jax.ShapeDtypeStruct(chunks.shape, chunks.dtype),
        in_specs=[vmem],
        out_specs=vmem,
        scratch_shapes=[
            pltpu.SemaphoreType.DMA((len(offsets),)),
            pltpu.SemaphoreType.DMA((len(offsets),)),
        ],
        compiler_params=pltpu.CompilerParams(collective_id=1, has_side_effects=True),
    )(chunks)
    return partial[:, 0, 1] + jnp.sum(received, axis=0)


def on_device(
    adjoint,
    forward,
    star_mats,
    flux_own,
    flux_neighbour,
    stiffness,
    projection,
    lifting,
    orientation,
    face_turn,
    mass_weights,
    param_mixing,
    neighbour,
    send_map,
    element_cell,
):
    cells = adjoint.shape[3]
    basis = adjoint.shape[2]
    slots = send_map.shape[1]
    face_basis = projection.shape[0] // 4
    curve_count = lax.axis_size("curve")
    group_count = lax.axis_size("grp")
    my_curve = lax.axis_index("curve")
    my_group = lax.axis_index("grp")
    f32 = jnp.float32

    own_flux = jnp.transpose(flux_own, (1, 0, 2))
    far_flux = jnp.transpose(flux_neighbour, (1, 0, 2))
    face_proj = projection.reshape(4, face_basis, basis)
    rows = 9 * face_basis

    faces = jnp.arange(4 * cells, dtype=jnp.int32)
    send_oh = (faces[:, None] == jnp.concatenate([send_map[0], send_map[1]])[None, :]).astype(f32)
    table_cols = jnp.arange(4 * cells + 2 * slots, dtype=jnp.int32)
    gather_oh = (table_cols[:, None] == neighbour.reshape(-1)[None, :]).astype(f32)

    mix = param_mixing.reshape(3, 9, 9)
    stiff_t = jnp.transpose(stiffness, (0, 2, 1))
    state = with_layout_constraint(
        adjoint.reshape(adjoint.shape[1:]), Layout((0, 1, 2))
    )
    density_sum = jnp.zeros((3, cells), f32)
    for time_step in range(STEPS):
        integral = predictor(state, stiffness, star_mats)
        own_trace = jnp.einsum("itb,qbc->qtic", face_proj, integral, precision=DENSE)
        table = own_trace.reshape(rows, 4 * cells)
        outgoing = jnp.dot(table, send_oh, precision=PRECISE)
        from_prev, from_next, volume_term = exchange(
            outgoing[:, slots:], outgoing[:, :slots], integral, stiff_t, star_mats
        )
        extended = jnp.concatenate([table, from_prev, from_next], axis=1)
        gathered = jnp.dot(extended, gather_oh, precision=PRECISE).reshape(9, face_basis, 4, cells)
        oriented = turn_faces(gathered, orientation, face_turn)
        face_flux = star(own_flux, own_trace) + star(far_flux, oriented)
        lifted = jnp.einsum("ibt,qtic->qbc", lifting, face_flux, precision=DENSE)
        state = state + volume_term - lifted
        weighted = state * mass_weights[None, :, None]
        mixed = jnp.einsum("pqr,rbc->pqbc", mix, forward[time_step, 0], precision=DENSE)
        density_sum = density_sum + jnp.sum(weighted[None] * mixed, axis=(1, 2))

    tile = element_cell // TILE
    inside = element_cell % TILE
    rel_group = (tile // curve_count - my_group) % group_count
    rel_curve = (tile % curve_count - my_curve + 1) % curve_count
    slot = (rel_group * 3 + rel_curve) * TILE + inside
    slot = jnp.where(rel_curve < 3, slot, -1)
    tile_oh = (slot[:, None] == jnp.arange(group_count * 3 * TILE, dtype=jnp.int32)[None, :]).astype(f32)
    partial = jnp.dot(density_sum, tile_oh, precision=PRECISE).reshape(3, group_count, 3, TILE)

    kernel = scatter_tiles(partial)
    return (state.reshape(adjoint.shape), kernel[None])


def solution(mesh):
    return jax.shard_map(
        on_device,
        mesh=mesh,
        in_specs=(
            P("grp", None, None, "curve"),
            P(None, "grp", None, None, "curve"),
            P(None, None, "curve"),
            P(None, None, "curve"),
            P(None, None, "curve"),
            P(),
            P(),
            P(),
            P(),
            P(None, "curve"),
            P(),
            P(),
            P(None, "curve"),
            P(None, "curve"),
            P("curve"),
        ),
        out_specs=(P("grp", None, None, "curve"), P(("grp", "curve"), None, None)),
        check_vma=False,
    )
```
